1024 devices in a mesh: section: 16 (over x, y_hi), dp: 4 (over y_lo, core), tensor: 16 (over z).
Axes of the slice: x: 4, y: 8 (y_hi: 4, y_lo: 2; y = y_hi * 2 + y_lo), z: 16, core: 2. Of those that a mesh axis runs over, the one named last changes fastest.
Arguments:
- queries: bfloat16 [8192, 8192], P(('section', 'dp'), 'tensor'), may hold values from -6 to 6
- images: bfloat16 [4, 3200, 8192], P('dp', 'section', 'tensor'), may hold values from -6 to 6
- kv_weight: bfloat16 [2, 8192, 1024], P(None, 'tensor', 'dp'), may hold values from -0.0625 to 0.0625
- q_gain: float32 [128], replicated, may hold values from 1 to 10
- k_gain: float32 [128], replicated, may hold values from 0.1 to 1.9
- tile_mask: int32 [8192, 4], P(('section', 'dp')), may hold values 0 or 1
Outputs:
- context: bfloat16 [8192, 8192], P(('section', 'dp'), 'tensor')
The draws below stay inside these ranges and needn't reach their ends.
All inputs are finite; a program needn't handle non-finite values. No bound on the sum of `tile_mask` on one device may be relied on, other than what follows from the above.
Results may differ from the reference program's by a relative error of at most 0.04.
Values may be sent and summed in bfloat16 or wider, within the bound.
A program may use at most 32 MiB of HBM per device.

```python
import math
import jax
import jax.numpy as jnp
from jax import lax

D = 8192
HD = 128
TILES = 4
TOK_DEV = 128
HQ = 64
KVH = 8
IMG = 3200
IMAGES = 4
TOKENS = 8192
N_SECTION = 16
N_DP = 4
N_TENSOR = 16


def draw_q_gain(key, part):
    lower = math.log(1.0)
    upper = math.log(4.0)
    return jnp.exp(jax.random.uniform(key, (HD,), jnp.float32, lower, upper))


def set_ends(drawn, key, smallest, top_value):
    dims = drawn.shape
    index_at = [jax.random.randint(jax.random.fold_in(key, axis), (), 0, dims[axis]) for axis in range(len(dims))]
    drawn = drawn.at[tuple(index_at)].set(smallest)
    longest = dims.index(max(dims))
    index_at[longest] = (index_at[longest] + 1) % dims[longest]
    return drawn.at[tuple(index_at)].set(top_value)


def block_levels(own_key, extent, split, smallest, high):
    level = 1.0
    for position, blocks in split:
        draws = jax.random.uniform(jax.random.fold_in(jax.random.fold_in(own_key, 6), position), (blocks,), jnp.float32, smallest / len(split), high / len(split))
        level = level * jnp.repeat(jnp.exp(draws), extent[position] // blocks).reshape((-1,) + (1,) * (len(extent) - 1 - position))
    return level


def noise(rng, dims, scale, bound, shards=(), held_as=jnp.bfloat16):
    drawn = jax.random.normal(rng, dims, jnp.float32) * scale
    if len(shards) > 0:
        drawn = block_levels(rng, dims, shards, -0.22, 0.18) * drawn
    return jnp.clip(drawn, min=-bound, max=bound).astype(held_as)


def setup_inputs(seed: int = 0) -> dict:
    splits = jax.random.split(jax.random.key(seed), 7)
    queries = noise(splits[0], (TOKENS, HQ * HD), 1.0, 6.0, ((0, 64), (1, 16)))
    images = noise(splits[1], (IMAGES, IMG, D), 1.0, 6.0, ((0, 4), (1, 16), (2, 16)))
    kv_weight = noise(splits[2], (2, D, KVH * HD), D ** -0.5, 0.0625, ((1, 16), (2, 4)))
    q_gain = draw_q_gain(jax.random.fold_in(splits[6], 71), 0)
    k_gain = jnp.clip(1.0 + 0.18 * jax.random.normal(splits[4], (HD,), jnp.float32), 0.1, 1.9)
    tile_mask = set_ends((jax.random.randint(splits[5], (TOKENS, TILES), 0, 4) < 3).astype(jnp.int32), jax.random.fold_in(splits[5], 1), 0, 1)
    return {"queries": queries, "images": images, "kv_weight": kv_weight, "q_gain": q_gain, "k_gain": k_gain, "tile_mask": tile_mask}


EPSILON = 1e-05
MASKED_SCORE = -1e+30

def normalize(values, gain_vec):
    mean_sq = lax.optimization_barrier(jnp.mean(values * values, axis=-1, keepdims=True))
    return values * lax.rsqrt(mean_sq + EPSILON) * gain_vec

def reference(queries, images, kv_weight, q_gain, k_gain, tile_mask):
    kv_width = KVH * HD
    cat_weight = jnp.concatenate([kv_weight[0], kv_weight[1]], axis=1)
    block_len = D // N_TENSOR
    q_all = queries.reshape(N_SECTION, N_DP, TOK_DEV, HQ, HD)
    mask_all = tile_mask.reshape(N_SECTION, N_DP, TOK_DEV, TILES)
    tile_len = IMG // TILES
    key_tile = jnp.arange(IMG, dtype=jnp.int32) // tile_len
    group_size = HQ // KVH
    results = []
    for image_idx in range(N_DP):
        features = images[image_idx]
        summed = jnp.zeros((IMG, 2 * kv_width), jnp.float32)
        for shard_idx in range(N_TENSOR):
            partial_value = jnp.dot(features[:, shard_idx * block_len:(shard_idx + 1) * block_len], cat_weight[shard_idx * block_len:(shard_idx + 1) * block_len], preferred_element_type=jnp.float32)
            summed = summed + lax.optimization_barrier(partial_value.astype(jnp.bfloat16)).astype(jnp.float32)
        key_rows = normalize(summed[:, :kv_width].reshape(IMG, KVH, HD), k_gain).astype(jnp.bfloat16)
        value_rows = summed[:, kv_width:].reshape(IMG, KVH, HD).astype(jnp.bfloat16)
        query_rows = q_all[:, image_idx].reshape(-1, HQ, HD).astype(jnp.float32)
        q_normed = (normalize(query_rows, q_gain) * HD ** (-0.5)).astype(jnp.bfloat16)
        tile_rows = mask_all[:, image_idx].reshape(-1, TILES)
        visible = jnp.take(tile_rows, key_tile, axis=1) > 0
        has_any = lax.optimization_barrier(jnp.sum(tile_rows, axis=1)) > 0

        def one_head(head_idx):
            q_head = lax.dynamic_index_in_dim(q_normed, head_idx, 1, keepdims=False)
            kv_idx = head_idx // group_size
            key_head = lax.dynamic_index_in_dim(key_rows, kv_idx, 1, keepdims=False)
            value_head = lax.dynamic_index_in_dim(value_rows, kv_idx, 1, keepdims=False)
            scores = jnp.dot(q_head, key_head.T, preferred_element_type=jnp.float32)
            row_top = lax.optimization_barrier(jnp.max(jnp.where(visible, scores, MASKED_SCORE), axis=1, keepdims=True))
            probabilities = jnp.where(visible, jnp.exp(scores - row_top), 0.0)
            row_total = lax.optimization_barrier(jnp.sum(probabilities, axis=1))
            mixture = jnp.dot(probabilities.astype(jnp.bfloat16), value_head, preferred_element_type=jnp.float32)
            divided = mixture / jnp.where(has_any, row_total, 1.0)[:, None]
            return jnp.where(has_any[:, None], divided, 0.0).astype(jnp.bfloat16)
        heads_out = lax.map(one_head, jnp.arange(HQ, dtype=jnp.int32))
        results.append(jnp.transpose(heads_out, (1, 0, 2)).reshape(N_SECTION, TOK_DEV, HQ * HD))
    return jnp.stack(results, axis=1).reshape(TOKENS, HQ * HD)
```

```python
import functools

import jax
import jax.numpy as jnp
from jax import lax
from jax.experimental import pallas as pl
from jax.experimental.pallas import tpu as pltpu
from jax.sharding import PartitionSpec as P

EPSILON = 1e-05
MASKED_SCORE = -1e30
MESH = pl.DeviceIdType.MESH
HD = 128
SPLIT = 96
UNIT = 104


def kernel(
    dims,
    img_hbm, w_hbm, q_hbm, qg_ref, kg_ref, mask_ref,
    out_ref,
    img, wbuf, qbuf, qs, bias, part, rp, rm, kv, scores, acc, top, total,
    load_sem, w_send, w_recv, p_send, p_recv, m_send, m_recv,
    kv_recv, z_send, y_relay, col_y, col_x, x_relay,
):
    n_x, n_y, n_t, heads = dims
    half_ring = n_t // 2
    s, d, t = lax.axis_index("section"), lax.axis_index("dp"), lax.axis_index("tensor")
    x, yh = s // n_y, s % n_y
    yl, core = d // 2, d % 2
    par = t % 2

    def section(a, b):
        return lax.rem(a + n_x, n_x) * n_y + lax.rem(b + n_y, n_y)

    partner = {"dp": d + 1 - 2 * core}
    y_next = {"section": section(x, yh + yl), "dp": (1 - yl) * 2 + core}
    y_prev = {"section": section(x, yh + yl - 1), "dp": (1 - yl) * 2 + core}
    z_next, z_prev = {"tensor": lax.rem(t + 1, n_t)}, {"tensor": lax.rem(t + n_t - 1, n_t)}
    z_pair = {"tensor": t + 1 - 2 * par}
    yh_next, yh_prev = {"section": section(x, yh + 1)}, {"section": section(x, yh - 1)}
    x_next, x_prev = {"section": section(x + 1, yh)}, {"section": section(x - 1, yh)}

    def remote(src, dst, send, recv, where):
        return pltpu.make_async_remote_copy(
            src_ref=src, dst_ref=dst, send_sem=send, recv_sem=recv, device_id=where, device_id_type=MESH
        )

    load_w = pltpu.make_async_copy(w_hbm, wbuf.at[d], load_sem.at[0])
    load_i = pltpu.make_async_copy(img_hbm.at[0], img, load_sem.at[1])
    load_q = pltpu.make_async_copy(q_hbm, qbuf, load_sem.at[2])
    load_w.start()
    load_i.start()
    load_q.start()

    barrier = pltpu.get_barrier_semaphore()
    near = (partner, y_next, y_prev, z_next, z_prev, yh_next, yh_prev, x_next, x_prev)
    for where in near:
        pl.semaphore_signal(barrier, inc=1, device_id=where, device_id_type=MESH)
    pl.semaphore_wait(barrier, len(near))

    other, far = d + 1 - 2 * core, (1 - yl) * 2 + core
    across = (1 - yl) * 2 + 1 - core
    w_far_k = remote(w_hbm.at[0], wbuf.at[d, 0], w_send.at[0], w_recv.at[0], y_next)
    w_far_v = remote(w_hbm.at[1], wbuf.at[d, 1], w_send.at[1], w_recv.at[1], y_prev)
    w_own = remote(w_hbm, wbuf.at[d], w_send.at[2], w_recv.at[2], partner)
    w_far_k.start()
    w_far_v.start()
    w_own.start()

    load_i.wait()
    load_w.wait()
    features = img[...]

    def project(group):
        for j in range(2):
            both = jnp.dot(features, wbuf[group, j], preferred_element_type=jnp.float32).astype(jnp.bfloat16)
            part[2 * group, j] = both[:, :HD]
            part[2 * group + 1, j] = both[:, HD:]

    project(d)

    load_q.wait()
    for h in range(heads):
        rows = qbuf[:, h * HD : (h + 1) * HD].astype(jnp.float32)
        mean_sq = jnp.mean(rows * rows, axis=-1, keepdims=True)
        normed = rows * lax.rsqrt(mean_sq + EPSILON) * qg_ref[...] * HD ** (-0.5)
        qs[h * HD : (h + 1) * HD, :] = normed.astype(jnp.bfloat16)
    tokens = mask_ref.shape[0]
    eye = (
        lax.broadcasted_iota(jnp.int32, (tokens, tokens), 0) == lax.broadcasted_iota(jnp.int32, (tokens, tokens), 1)
    ).astype(jnp.float32)
    seen = lax.dot_general(
        mask_ref[...].astype(jnp.float32), eye, (((0,), (0,)), ((), ())), preferred_element_type=jnp.float32
    )
    hidden = jnp.where(seen > 0.5, 0.0, MASKED_SCORE)
    for h in range(heads):
        bias[0:n_x, h * HD : (h + 1) * HD] = hidden
    top[...] = jnp.full_like(top, MASKED_SCORE)
    total[...] = jnp.zeros_like(total)
    acc[...] = jnp.zeros_like(acc)

    remote(w_hbm, wbuf.at[other], w_send.at[2], w_recv.at[2], partner).wait_recv()
    project(other)
    fwd = []
    for j in range(2):
        remote(w_hbm.at[j], wbuf.at[far, j], w_send.at[j], w_recv.at[j], partner).wait_recv()
        copy = remote(wbuf.at[far, j], wbuf.at[far, j], w_send.at[3 + j], w_recv.at[3 + j], partner)
        copy.start()
        fwd.append(copy)
    project(far)
    for j in range(2):
        remote(wbuf.at[far, j], wbuf.at[across, j], w_send.at[3 + j], w_recv.at[3 + j], partner).wait_recv()
    project(across)

    def own_part(u, j):
        start = pl.multiple_of(lax.rem(u, 2) * SPLIT, 16)
        return part.at[lax.div(u, 2), j, pl.ds(start, UNIT), :]

    sent = []
    for k in range(half_ring):
        for j in range(2):
            u = lax.rem(t + half_ring - k, n_t)
            if k == 0:
                src = own_part(u, j)
            else:
                src = rp.at[k - 1, j]
                remote(src, src, p_send.at[k - 1, j], p_recv.at[k - 1, j], z_next).wait_recv()
                src[...] = (src[...].astype(jnp.float32) + own_part(u, j)[...].astype(jnp.float32)).astype(jnp.bfloat16)
            copy = remote(src, rp.at[k, j], p_send.at[k, j], p_recv.at[k, j], z_next)
            copy.start()
            sent.append(copy)
            if k < half_ring - 1:
                u = lax.rem(t + half_ring + 1 + k, n_t)
                if k == 0:
                    src = own_part(u, j)
                else:
                    src = rm.at[k - 1, j]
                    remote(src, src, m_send.at[k - 1, j], m_recv.at[k - 1, j], z_prev).wait_recv()
                    src[...] = (src[...].astype(jnp.float32) + own_part(u, j)[...].astype(jnp.float32)).astype(
                        jnp.bfloat16
                    )
                copy = remote(src, rm.at[k, j], m_send.at[k, j], m_recv.at[k, j], z_prev)
                copy.start()
                sent.append(copy)

    for j in range(2):
        last_p, last_m = rp.at[half_ring - 1, j], rm.at[half_ring - 2, j]
        remote(last_m, last_m, m_send.at[half_ring - 2, j], m_recv.at[half_ring - 2, j], z_prev).wait_recv()
        remote(last_p, last_p, p_send.at[half_ring - 1, j], p_recv.at[half_ring - 1, j], z_next).wait_recv()
        rows = (
            own_part(t, j)[...].astype(jnp.float32)
            + last_p[...].astype(jnp.float32)
            + last_m[...].astype(jnp.float32)
        )
        if j == 0:
            mean_sq = jnp.mean(rows * rows, axis=-1, keepdims=True)
            rows = rows * lax.rsqrt(mean_sq + EPSILON) * kg_ref[...]
        kv[x, yh, par, j] = rows.astype(jnp.bfloat16)

    def place(a, b):
        return lax.rem(a + n_x, n_x), lax.rem(b + n_y, n_y)

    def chunk(a, b, q, send, where):
        a, b = place(a, b)
        return remote(kv.at[a, b, q], kv.at[a, b, q], send, kv_recv.at[a, b, q], where)

    def arrived(a, b, q):
        chunk(a, b, q, z_send, z_pair).wait_recv()

    def send_column(slot, b, q, i):
        for direction, where in enumerate((x_next, x_prev)):
            chunk(x, b, q, col_x.at[slot, i, direction], where).start()

    chunk(x, yh, par, z_send, z_pair).start()
    for i, q in enumerate((par, 1 - par)):
        if i == 1:
            arrived(x, yh, q)
        chunk(x, yh, q, col_y.at[i, 0], yh_next).start()
        chunk(x, yh, q, col_y.at[i, 1], yh_prev).start()
        send_column(0, yh, q, i)
    for i, q in enumerate((par, 1 - par)):
        arrived(x, yh - 1, q)

        @pl.when(q == 0)
        def _():
            chunk(x, yh - 1, 0, y_relay.at[0], yh_next).start()

        send_column(1, yh - 1, q, i)
        arrived(x, yh + 1, q)

        @pl.when(q == 1)
        def _():
            chunk(x, yh + 1, 1, y_relay.at[1], yh_prev).start()

        send_column(2, yh + 1, q, i)
    for q in range(2):
        arrived(x, yh + 2, q)
        send_column(3, yh + 2, q, q)

    def offset(n):
        return jnp.where(n == 0, 0, jnp.where(n == 1, 3, n - 1))

    def attend(i, carry):
        inner = (i >= 2) & (i < 6)
        own = i < 2
        base = jnp.where(own, 2 * i, 2 * (i - 6))
        slot_a = jnp.where(inner, i - 2, base)
        slot_b = jnp.where(inner, i - 2, base + 1)
        xa = jnp.where(own, x, jnp.where(inner, x - 1, x + 2))
        xb = jnp.where(own, x, jnp.where(inner, x + 1, x + 2))
        xa, ya = place(xa, yh + offset(slot_a))
        xb, yb = place(xb, yh + offset(slot_b))

        @pl.when(i >= 2)
        def _():
            for q in (par, 1 - par):
                arrived(xa, ya, q)

                @pl.when(inner & (q == 0))
                def _():
                    chunk(xa, ya, 0, x_relay.at[slot_a, 0], x_next).start()

                arrived(xb, yb, q)

                @pl.when(inner & (q == 1))
                def _():
                    chunk(xb, yb, 1, x_relay.at[slot_b, 1], x_prev).start()

        queries = qs[...]
        best = top[...]
        for n, (a, b) in enumerate(((xa, ya), (xb, yb))):
            keys = jnp.concatenate([kv[a, b, 0, 0][:SPLIT], kv[a, b, 1, 0]], axis=0)
            found = lax.dot_general(
                keys, queries, (((1,), (1,)), ((), ())), preferred_element_type=jnp.float32
            ) + bias[pl.ds(a, 1), :]
            scores[n] = found
            best = jnp.maximum(best, jnp.max(found, axis=0, keepdims=True))
        scale = jnp.exp(top[...] - best)
        top[...] = best
        row_sum = total[...] * scale
        added = acc[...] * scale
        for n, (a, b) in enumerate(((xa, ya), (xb, yb))):
            weights = jnp.exp(scores[n] - best)
            row_sum = row_sum + jnp.sum(weights, axis=0, keepdims=True)
            values = jnp.concatenate([kv[a, b, 0, 1][:SPLIT], kv[a, b, 1, 1]], axis=0)
            added = added + lax.dot_general(
                values, weights.astype(jnp.bfloat16), (((0,), (0,)), ((), ())), preferred_element_type=jnp.float32
            )
        total[...] = row_sum
        acc[...] = added
        return carry

    lax.fori_loop(0, 8, attend, 0)

    has_any = jnp.max(bias[0:n_x, :], axis=0, keepdims=True) > 0.5 * MASKED_SCORE
    divided = acc[...] / jnp.where(has_any, total[...], 1.0)
    context = jnp.where(has_any, divided, 0.0)
    for h in range(heads):
        out_ref[:, h * HD : (h + 1) * HD] = context[:, h * HD : (h + 1) * HD].T.astype(jnp.bfloat16)

    for copy in [w_far_k, w_far_v, w_own] + fwd + sent:
        copy.wait_send()
    chunk(x, yh, par, z_send, z_pair).wait_send()
    for i in range(2):
        for direction in range(2):
            chunk(x, yh, i, col_y.at[i, direction], yh_next).wait_send()
            for slot in range(4):
                chunk(x, yh, i, col_x.at[slot, i, direction], x_next).wait_send()
        chunk(x, yh, i, y_relay.at[i], yh_next).wait_send()
        for slot in range(4):
            chunk(x, yh, i, x_relay.at[slot, i], x_next).wait_send()


def solution(mesh):
    n_x = n_y = 4
    n_t = mesh.shape["tensor"]

    def on_device(queries, images, kv_weight, q_gain, k_gain, tile_mask):
        tokens, width = queries.shape
        rows, depth = images.shape[1:]
        heads = width // HD
        groups = mesh.shape["dp"]
        any_space = pl.BlockSpec(memory_space=pl.ANY)
        vmem = pl.BlockSpec(memory_space=pltpu.VMEM)
        dma = pltpu.SemaphoreType.DMA
        return pl.pallas_call(
            functools.partial(kernel, (n_x, n_y, n_t, heads)),
            out_shape=jax.ShapeDtypeStruct((tokens, width), jnp.bfloat16),
            in_specs=[any_space, any_space, any_space, vmem, vmem, vmem],
            out_specs=vmem,
            scratch_shapes=[
                pltpu.VMEM((rows, depth), jnp.bfloat16),
                pltpu.VMEM((groups, *kv_weight.shape), jnp.bfloat16),
                pltpu.VMEM((tokens, width), jnp.bfloat16),
                pltpu.VMEM((width, HD), jnp.bfloat16),
                pltpu.VMEM((8, width), jnp.float32),
                pltpu.VMEM((n_t // 2, 2, rows, HD), jnp.bfloat16),
                pltpu.VMEM((n_t // 2, 2, UNIT, HD), jnp.bfloat16),
                pltpu.VMEM((n_t // 2 - 1, 2, UNIT, HD), jnp.bfloat16),
                pltpu.VMEM((n_x, n_y, 2, 2, UNIT, HD), jnp.bfloat16),
                pltpu.VMEM((2, rows, width), jnp.float32),
                pltpu.VMEM((HD, width), jnp.float32),
                pltpu.VMEM((1, width), jnp.float32),
                pltpu.VMEM((1, width), jnp.float32),
                dma((3,)), dma((5,)), dma((5,)),
                dma((n_t // 2, 2)), dma((n_t // 2, 2)),
                dma((n_t // 2 - 1, 2)), dma((n_t // 2 - 1, 2)),
                dma((n_x, n_y, 2)), dma, dma((2,)),
                dma((2, 2)), dma((4, 2, 2)), dma((4, 2)),
            ],
            compiler_params=pltpu.CompilerParams(
                collective_id=0, has_side_effects=True, vmem_limit_bytes=40 * 1024 * 1024
            ),
        )(images, kv_weight, queries, q_gain.reshape(1, HD), k_gain.reshape(1, HD), tile_mask)

    in_specs = (
        P(("section", "dp"), "tensor"),
        P("dp", "section", "tensor"),
        P(None, "tensor", "dp"),
        P(),
        P(),
        P(("section", "dp"), None),
    )
    out_specs = P(("section", "dp"), "tensor")
    return jax.shard_map(on_device, mesh=mesh, in_specs=in_specs, out_specs=out_specs, check_vma=False)
```

```python
import functools

import jax
import jax.numpy as jnp
from jax import lax
from jax.experimental import pallas as pl
from jax.experimental.pallas import tpu as pltpu
from jax.sharding import PartitionSpec as P

EPSILON = 1e-05
MASKED_SCORE = -1e30
MESH = pl.DeviceIdType.MESH
HD = 128
SPLIT = 96
UNIT = 104


def kernel(
    dims,
    img_hbm, w_hbm, q_hbm, qg_ref, kg_ref, mask_ref,
    out_ref,
    img, wbuf, qbuf, qs, bias, part, rp, rm, kv, scores, acc, top, total,
    load_sem, w_send, w_recv, p_send, p_recv, m_send, m_recv,
    kv_recv, z_send, y_relay, col_y, col_x, x_relay,
):
    n_x, n_y, n_t, heads = dims
    half_ring = n_t // 2
    s, d, t = lax.axis_index("section"), lax.axis_index("dp"), lax.axis_index("tensor")
    x, yh = s // n_y, s % n_y
    yl, core = d // 2, d % 2
    par = t % 2

    def section(a, b):
        return lax.rem(a + n_x, n_x) * n_y + lax.rem(b + n_y, n_y)

    partner = {"dp": d + 1 - 2 * core}
    y_next = {"section": section(x, yh + yl), "dp": (1 - yl) * 2 + core}
    y_prev = {"section": section(x, yh + yl - 1), "dp": (1 - yl) * 2 + core}
    z_near = tuple({"tensor": lax.rem(t + n_t + step, n_t)} for step in (-2, -1, 1, 2))
    z_pair = {"tensor": t + 1 - 2 * par}
    yh_next, yh_prev = {"section": section(x, yh + 1)}, {"section": section(x, yh - 1)}
    x_next, x_prev = {"section": section(x + 1, yh)}, {"section": section(x - 1, yh)}

    def remote(src, dst, send, recv, where):
        return pltpu.make_async_remote_copy(
            src_ref=src, dst_ref=dst, send_sem=send, recv_sem=recv, device_id=where, device_id_type=MESH
        )

    load_w = pltpu.make_async_copy(w_hbm, wbuf.at[d], load_sem.at[0])
    load_i = pltpu.make_async_copy(img_hbm.at[0], img, load_sem.at[1])
    load_q = pltpu.make_async_copy(q_hbm, qbuf, load_sem.at[2])
    load_w.start()
    load_i.start()
    load_q.start()

    barrier = pltpu.get_barrier_semaphore()
    near = (partner, y_next, y_prev, *z_near, yh_next, yh_prev, x_next, x_prev)
    for where in near:
        pl.semaphore_signal(barrier, inc=1, device_id=where, device_id_type=MESH)
    pl.semaphore_wait(barrier, len(near))

    other, far = d + 1 - 2 * core, (1 - yl) * 2 + core
    across = (1 - yl) * 2 + 1 - core
    w_far_k = remote(w_hbm.at[0], wbuf.at[d, 0], w_send.at[0], w_recv.at[0], y_next)
    w_far_v = remote(w_hbm.at[1], wbuf.at[d, 1], w_send.at[1], w_recv.at[1], y_prev)
    w_own = remote(w_hbm, wbuf.at[d], w_send.at[2], w_recv.at[2], partner)
    w_far_k.start()
    w_far_v.start()
    w_own.start()

    load_i.wait()
    load_w.wait()
    features = img[...]

    def project(group):
        for j in range(2):
            both = jnp.dot(features, wbuf[group, j], preferred_element_type=jnp.float32).astype(jnp.bfloat16)
            part[2 * group, j] = both[:, :HD]
            part[2 * group + 1, j] = both[:, HD:]

    project(d)

    load_q.wait()
    for h in range(heads):
        rows = qbuf[:, h * HD : (h + 1) * HD].astype(jnp.float32)
        mean_sq = jnp.mean(rows * rows, axis=-1, keepdims=True)
        normed = rows * lax.rsqrt(mean_sq + EPSILON) * qg_ref[...] * HD ** (-0.5)
        qs[h * HD : (h + 1) * HD, :] = normed.astype(jnp.bfloat16)
    hidden = jnp.where(mask_ref[...] > 0, 0.0, MASKED_SCORE)
    for h in range(heads):
        bias[0:n_x, h * HD : (h + 1) * HD] = hidden
    top[...] = jnp.full_like(top, MASKED_SCORE)
    total[...] = jnp.zeros_like(total)
    acc[...] = jnp.zeros_like(acc)

    remote(w_hbm, wbuf.at[other], w_send.at[2], w_recv.at[2], partner).wait_recv()
    project(other)
    fwd = []
    for j in range(2):
        remote(w_hbm.at[j], wbuf.at[far, j], w_send.at[j], w_recv.at[j], partner).wait_recv()
        copy = remote(wbuf.at[far, j], wbuf.at[far, j], w_send.at[3 + j], w_recv.at[3 + j], partner)
        copy.start()
        fwd.append(copy)
    project(far)
    for j in range(2):
        remote(wbuf.at[far, j], wbuf.at[across, j], w_send.at[3 + j], w_recv.at[3 + j], partner).wait_recv()
    project(across)

    def own_part(u, j):
        start = pl.multiple_of(lax.rem(u, 2) * SPLIT, 16)
        return part.at[lax.div(u, 2), j, pl.ds(start, UNIT), :]

    sent = []
    rings = ((1, half_ring, rp, p_send, p_recv), (-1, half_ring - 1, rm, m_send, m_recv))

    def hop(ring, offset, j, src):
        sign, _, buf, send, recv = rings[ring]
        jump = 2 - offset % 2
        where = {"tensor": lax.rem(t + n_t + sign * jump, n_t)}
        return remote(src, buf.at[offset - 1, j], send.at[offset - 1, j], recv.at[offset - 1, j], where)

    def send_sum(ring, offset, j):
        sign, longest, buf, send, recv = rings[ring]
        own = own_part(lax.rem(t + n_t + sign * offset, n_t), j)
        src = own
        if offset % 2 == 0 and offset < longest:
            rows = own[...].astype(jnp.float32)
            for before in (offset + 1, offset + 2):
                if before <= longest:
                    got = buf.at[before - 1, j]
                    hop(ring, before, j, got).wait_recv()
                    rows = rows + got[...].astype(jnp.float32)
            src = buf.at[offset + 1 if offset + 2 <= longest else offset, j]
            src[...] = rows.astype(jnp.bfloat16)
        copy = hop(ring, offset, j, src)
        copy.start()
        sent.append(copy)

    for offset in range(half_ring, 0, -2):
        for j in range(2):
            for ring in range(2):
                for now in (offset, offset - 1):
                    if now <= rings[ring][1]:
                        send_sum(ring, now, j)

    for j in range(2):
        rows = own_part(t, j)[...].astype(jnp.float32)
        for ring in range(2):
            for offset in (1, 2):
                got = rings[ring][2].at[offset - 1, j]
                hop(ring, offset, j, got).wait_recv()
                rows = rows + got[...].astype(jnp.float32)
        if j == 0:
            mean_sq = jnp.mean(rows * rows, axis=-1, keepdims=True)
            rows = rows * lax.rsqrt(mean_sq + EPSILON) * kg_ref[...]
        kv[x, yh, par, j] = rows.astype(jnp.bfloat16)

    def place(a, b):
        return lax.rem(a + n_x, n_x), lax.rem(b + n_y, n_y)

    def chunk(a, b, q, send, where):
        a, b = place(a, b)
        return remote(kv.at[a, b, q], kv.at[a, b, q], send, kv_recv.at[a, b, q], where)

    def arrived(a, b, q):
        chunk(a, b, q, z_send, z_pair).wait_recv()

    def send_column(slot, b, q, i):
        for direction, where in enumerate((x_next, x_prev)):
            chunk(x, b, q, col_x.at[slot, i, direction], where).start()

    chunk(x, yh, par, z_send, z_pair).start()
    for i, q in enumerate((par, 1 - par)):
        if i == 1:
            arrived(x, yh, q)
        chunk(x, yh, q, col_y.at[i, 0], yh_next).start()
        chunk(x, yh, q, col_y.at[i, 1], yh_prev).start()
        send_column(0, yh, q, i)
    for i, q in enumerate((par, 1 - par)):
        arrived(x, yh - 1, q)

        @pl.when(q == 0)
        def _():
            chunk(x, yh - 1, 0, y_relay.at[0], yh_next).start()

        send_column(1, yh - 1, q, i)
        arrived(x, yh + 1, q)

        @pl.when(q == 1)
        def _():
            chunk(x, yh + 1, 1, y_relay.at[1], yh_prev).start()

        send_column(2, yh + 1, q, i)
    for q in range(2):
        arrived(x, yh + 2, q)
        send_column(3, yh + 2, q, q)

    def offset(n):
        return jnp.where(n == 0, 0, jnp.where(n == 1, 3, n - 1))

    def attend(i, carry):
        inner = (i >= 2) & (i < 6)
        own = i < 2
        base = jnp.where(own, 2 * i, 2 * (i - 6))
        slot_a = jnp.where(inner, i - 2, base)
        slot_b = jnp.where(inner, i - 2, base + 1)
        xa = jnp.where(own, x, jnp.where(inner, x - 1, x + 2))
        xb = jnp.where(own, x, jnp.where(inner, x + 1, x + 2))
        xa, ya = place(xa, yh + offset(slot_a))
        xb, yb = place(xb, yh + offset(slot_b))

        @pl.when(i >= 2)
        def _():
            for q in (par, 1 - par):
                arrived(xa, ya, q)

                @pl.when(inner & (q == 0))
                def _():
                    chunk(xa, ya, 0, x_relay.at[slot_a, 0], x_next).start()

                arrived(xb, yb, q)

                @pl.when(inner & (q == 1))
                def _():
                    chunk(xb, yb, 1, x_relay.at[slot_b, 1], x_prev).start()

        queries = qs[...]
        best = top[...]
        for n, (a, b) in enumerate(((xa, ya), (xb, yb))):
            keys = jnp.concatenate([kv[a, b, 0, 0][:SPLIT], kv[a, b, 1, 0]], axis=0)
            found = lax.dot_general(
                keys, queries, (((1,), (1,)), ((), ())), preferred_element_type=jnp.float32
            ) + bias[pl.ds(a, 1), :]
            scores[n] = found
            best = jnp.maximum(best, jnp.max(found, axis=0, keepdims=True))
        scale = jnp.exp(top[...] - best)
        top[...] = best
        row_sum = total[...] * scale
        added = acc[...] * scale
        for n, (a, b) in enumerate(((xa, ya), (xb, yb))):
            weights = jnp.exp(scores[n] - best)
            row_sum = row_sum + jnp.sum(weights, axis=0, keepdims=True)
            values = jnp.concatenate([kv[a, b, 0, 1][:SPLIT], kv[a, b, 1, 1]], axis=0)
            added = added + lax.dot_general(
                values, weights.astype(jnp.bfloat16), (((0,), (0,)), ((), ())), preferred_element_type=jnp.float32
            )
        total[...] = row_sum
        acc[...] = added
        return carry

    lax.fori_loop(0, 8, attend, 0)

    has_any = jnp.max(bias[0:n_x, :], axis=0, keepdims=True) > 0.5 * MASKED_SCORE
    divided = acc[...] / jnp.where(has_any, total[...], 1.0)
    context = jnp.where(has_any, divided, 0.0)
    for h in range(heads):
        out_ref[:, h * HD : (h + 1) * HD] = context[:, h * HD : (h + 1) * HD].T.astype(jnp.bfloat16)

    for copy in [w_far_k, w_far_v, w_own] + fwd + sent:
        copy.wait_send()
    chunk(x, yh, par, z_send, z_pair).wait_send()
    for i in range(2):
        for direction in range(2):
            chunk(x, yh, i, col_y.at[i, direction], yh_next).wait_send()
            for slot in range(4):
                chunk(x, yh, i, col_x.at[slot, i, direction], x_next).wait_send()
        chunk(x, yh, i, y_relay.at[i], yh_next).wait_send()
        for slot in range(4):
            chunk(x, yh, i, x_relay.at[slot, i], x_next).wait_send()


def solution(mesh):
    n_x = n_y = 4
    n_t = mesh.shape["tensor"]

    def on_device(queries, images, kv_weight, q_gain, k_gain, tile_mask):
        tokens, width = queries.shape
        rows, depth = images.shape[1:]
        heads = width // HD
        groups = mesh.shape["dp"]
        any_space = pl.BlockSpec(memory_space=pl.ANY)
        vmem = pl.BlockSpec(memory_space=pltpu.VMEM)
        dma = pltpu.SemaphoreType.DMA
        return pl.pallas_call(
            functools.partial(kernel, (n_x, n_y, n_t, heads)),
            out_shape=jax.ShapeDtypeStruct((tokens, width), jnp.bfloat16),
            in_specs=[any_space, any_space, any_space, vmem, vmem, vmem],
            out_specs=vmem,
            scratch_shapes=[
                pltpu.VMEM((rows, depth), jnp.bfloat16),
                pltpu.VMEM((groups, *kv_weight.shape), jnp.bfloat16),
                pltpu.VMEM((tokens, width), jnp.bfloat16),
                pltpu.VMEM((width, HD), jnp.bfloat16),
                pltpu.VMEM((8, width), jnp.float32),
                pltpu.VMEM((n_t // 2, 2, rows, HD), jnp.bfloat16),
                pltpu.VMEM((n_t // 2, 2, UNIT, HD), jnp.bfloat16),
                pltpu.VMEM((n_t // 2 - 1, 2, UNIT, HD), jnp.bfloat16),
                pltpu.VMEM((n_x, n_y, 2, 2, UNIT, HD), jnp.bfloat16),
                pltpu.VMEM((2, rows, width), jnp.float32),
                pltpu.VMEM((HD, width), jnp.float32),
                pltpu.VMEM((1, width), jnp.float32),
                pltpu.VMEM((1, width), jnp.float32),
                dma((3,)), dma((5,)), dma((5,)),
                dma((n_t // 2, 2)), dma((n_t // 2, 2)),
                dma((n_t // 2 - 1, 2)), dma((n_t // 2 - 1, 2)),
                dma((n_x, n_y, 2)), dma, dma((2,)),
                dma((2, 2)), dma((4, 2, 2)), dma((4, 2)),
            ],
            compiler_params=pltpu.CompilerParams(
                collective_id=0, has_side_effects=True, vmem_limit_bytes=67043328
            ),
        )(images, kv_weight, queries, q_gain.reshape(1, HD), k_gain.reshape(1, HD), tile_mask.T)

    in_specs = (
        P(("section", "dp"), "tensor"),
        P("dp", "section", "tensor"),
        P(None, "tensor", "dp"),
        P(),
        P(),
        P(("section", "dp"), None),
    )
    out_specs = P(("section", "dp"), "tensor")
    return jax.shard_map(on_device, mesh=mesh, in_specs=in_specs, out_specs=out_specs, check_vma=False)
```

```python
import functools
import math

import jax
import jax.numpy as jnp
from jax import lax
from jax.experimental import pallas as pl
from jax.experimental.pallas import tpu as pltpu
from jax.sharding import PartitionSpec as P

EPSILON = 1e-05
MASKED_SCORE = -1e30
LOGICAL = pl.DeviceIdType.LOGICAL
HD = 128
SPLIT = 96
UNIT = 104
SENDS = 72


def kernel(
    dims,
    img_hbm, w_hbm, q_hbm, qg_hbm, kg_hbm, mask_hbm,
    out_ref,
    img, wbuf, qbuf, qg_ref, kg_ref, mask_ref, qs, bias, part, rp, rm, kv, scores, acc, top, total,
    load_sem, w_send, w_recv, p_send, p_recv, m_send, m_recv, kv_recv, kv_send,
):
    n_x, n_y, n_t, heads, strides = dims
    strides = dict(strides)
    half_ring = n_t // 2
    s, d, t = lax.axis_index("section"), lax.axis_index("dp"), lax.axis_index("tensor")
    x, yh = s // n_y, s % n_y
    yl, core = d // 2, d % 2
    par = t % 2

    def wrap(value, size):
        return jnp.where(value >= size, value - size, value)

    near_x = tuple(wrap(x + step, n_x) for step in range(4))
    near_y = tuple(wrap(yh + step, n_y) for step in range(4))

    def device(a=0, b=0, dp=None, tensor=None):
        section = near_x[a % 4] * n_y + near_y[b % 4]
        dp, tensor = d if dp is None else dp, t if tensor is None else tensor
        return section * strides["section"] + dp * strides["dp"] + tensor * strides["tensor"]

    other, far = d + 1 - 2 * core, (1 - yl) * 2 + core
    across = (1 - yl) * 2 + 1 - core
    low_side = device(dp=far)
    partner = device(dp=other)
    y_next = jnp.where(yl == 0, low_side, device(b=1, dp=far))
    y_prev = jnp.where(yl == 1, low_side, device(b=-1, dp=far))
    z_at = {step: device(tensor=wrap(t + step % n_t, n_t)) for step in (-2, -1, 1, 2)}
    z_pair = device(tensor=t + 1 - 2 * par)
    y_group = tuple(device(b=step) for step in (-1, 1, 2))
    x_group = tuple(device(a=step) for step in (-1, 1, 2))

    def remote(src, dst, send, recv, where):
        return pltpu.make_async_remote_copy(
            src_ref=src, dst_ref=dst, send_sem=send, recv_sem=recv, device_id=where, device_id_type=LOGICAL
        )

    loads = [
        pltpu.make_async_copy(src, dst, load_sem.at[i])
        for i, (src, dst) in enumerate(
            (
                (img_hbm.at[0], img),
                (w_hbm, wbuf.at[d]),
                (q_hbm, qbuf),
                (qg_hbm, qg_ref),
                (mask_hbm, mask_ref),
                (kg_hbm, kg_ref),
            )
        )
    ]
    for load in loads:
        load.start()

    barrier = pltpu.get_barrier_semaphore()
    near = (partner, y_next, y_prev, *z_at.values(), *y_group, *x_group)
    for where in near:
        pl.semaphore_signal(barrier, inc=1, device_id=where, device_id_type=LOGICAL)
    pl.semaphore_wait(barrier, len(near))

    depth = img.shape[1] // 2

    def halves(group, j, stage):
        rows = (pl.ds(0, depth), pl.ds(depth, depth))
        return [(wbuf.at[group, j, rows[i], :], w_send.at[stage, j, i], w_recv.at[stage, j, i]) for i in range(2)]

    sent = []

    def launch(copy):
        copy.start()
        sent.append(copy)

    for j in range(2):
        for i, where in enumerate((y_next, y_prev)):
            dst, send, recv = halves(d, j, 0)[i]
            launch(remote(w_hbm.at[j, pl.ds(i * depth, depth), :], dst, send, recv, where))
        launch(remote(w_hbm.at[j], wbuf.at[d, j], w_send.at[2, j, 0], w_recv.at[2, j, 0], partner))

    loads[0].wait()
    loads[1].wait()
    features = img[...]

    def project(group, j):
        both = jnp.dot(features, wbuf[group, j], preferred_element_type=jnp.float32).astype(jnp.bfloat16)
        part[2 * group, j] = both[:, :HD]
        part[2 * group + 1, j] = both[:, HD:]

    project(d, 0)
    project(d, 1)

    for load in loads[2:]:
        load.wait()
    for h in range(heads):
        rows = qbuf[:, h * HD : (h + 1) * HD].astype(jnp.float32)
        mean_sq = jnp.mean(rows * rows, axis=-1, keepdims=True)
        normed = rows * lax.rsqrt(mean_sq + EPSILON) * qg_ref[...] * HD ** (-0.5)
        qs[h * HD : (h + 1) * HD, :] = normed.astype(jnp.bfloat16)
    hidden = jnp.where(mask_ref[...] > 0, 0.0, MASKED_SCORE)
    for h in range(heads):
        bias[0:n_x, h * HD : (h + 1) * HD] = hidden
    top[...] = jnp.full_like(top, MASKED_SCORE)
    total[...] = jnp.zeros_like(total)
    acc[...] = jnp.zeros_like(acc)

    for j in range(2):
        remote(w_hbm.at[j], wbuf.at[other, j], w_send.at[2, j, 0], w_recv.at[2, j, 0], partner).wait_recv()
        project(other, j)

    def far_weights(j):
        for (dst, send, recv), (_, send_on, recv_on) in zip(halves(far, j, 0), halves(far, j, 1)):
            remote(dst, dst, send, recv, partner).wait_recv()
            launch(remote(dst, dst, send_on, recv_on, partner))
        project(far, j)
        for dst, send, recv in halves(across, j, 1):
            remote(dst, dst, send, recv, partner).wait_recv()
        project(across, j)

    pair, heads_kv = t // 2, n_t // 2

    def own_part(offset, j):
        offset %= n_t
        odd = offset % 2
        start = (1 - par if odd else par) * SPLIT
        head = wrap(pair + offset // 2 + (par if odd else 0), heads_kv)
        return part.at[head, j, pl.ds(pl.multiple_of(start, 16), UNIT), :]

    rings = ((1, half_ring, rp, p_send, p_recv), (-1, half_ring - 1, rm, m_send, m_recv))

    def hop(ring, offset, j, src):
        sign, _, buf, send, recv = rings[ring]
        jump = 2 - offset % 2
        return remote(src, buf.at[offset - 1, j], send.at[offset - 1, j], recv.at[offset - 1, j], z_at[sign * jump])

    def send_sum(ring, offset, j):
        sign, longest, buf, send, recv = rings[ring]
        own = own_part(sign * offset, j)
        src = own
        if offset % 2 == 0 and offset < longest:
            rows = own[...].astype(jnp.float32)
            for before in (offset + 1, offset + 2):
                if before <= longest:
                    got = buf.at[before - 1, j]
                    hop(ring, before, j, got).wait_recv()
                    rows = rows + got[...].astype(jnp.float32)
            src = buf.at[offset + 1 if offset + 2 <= longest else offset, j]
            src[...] = rows.astype(jnp.bfloat16)
        launch(hop(ring, offset, j, src))

    for offset in range(half_ring, 0, -2):
        for j in range(2):
            if offset == half_ring:
                far_weights(j)
            for ring in range(2):
                for now in (offset, offset - 1):
                    if now <= rings[ring][1]:
                        send_sum(ring, now, j)

    def finish(j):
        rows = own_part(0, j)[...].astype(jnp.float32)
        for ring in range(2):
            for offset in (1, 2):
                got = rings[ring][2].at[offset - 1, j]
                hop(ring, offset, j, got).wait_recv()
                rows = rows + got[...].astype(jnp.float32)
        if j == 0:
            mean_sq = jnp.mean(rows * rows, axis=-1, keepdims=True)
            rows = rows * lax.rsqrt(mean_sq + EPSILON) * kg_ref[...]
        kv[x, yh, par, j] = rows.astype(jnp.bfloat16)

    flying = []

    def chunk_at(a, b, q, j, send, where):
        return remote(kv.at[a, b, q, j], kv.at[a, b, q, j], send, kv_recv.at[a, b, q, j], where)

    def chunk(a, b, q, j, send, where):
        return chunk_at(near_x[a % 4], near_y[b % 4], q, j, send, where)

    def arrived(a, b, q, j):
        chunk(a, b, q, j, kv_send.at[0], z_pair).wait_recv()

    def arrived_at(a, b, q, j):
        chunk_at(a, b, q, j, kv_send.at[0], z_pair).wait_recv()

    def forward(a, b, q, j, *where):
        for device in where:
            chunk(a, b, q, j, kv_send.at[len(flying)], device).start()
            flying.append(j)

    both_j = (0, 1)
    opp = 1 - par
    for j in both_j:
        finish(j)
        forward(0, 0, par, j, z_pair, *y_group, *x_group)
    for j in both_j:
        arrived(0, 0, opp, j)
        forward(0, 0, opp, j, *y_group)
    for j in both_j:
        for step in (-1, 1, 2):
            arrived(step, 0, par, j)
            forward(step, 0, par, j, z_pair)
    for slot in (-1, 1, 2):
        for j in both_j:
            arrived(0, slot, par, j)
            forward(0, slot, par, j, *x_group)

    def events_at(i):
        @pl.when(i == 2)
        def _():
            for j in both_j:
                for step in (-1, 1, 2):
                    arrived(step, -1, par, j)
                    forward(step, -1, par, j, z_pair)
            for slot in (1, 2):
                for j in both_j:
                    arrived(0, slot, opp, j)
                    forward(0, slot, opp, j, *x_group)
            for j in both_j:
                for step in (-1, 1, 2):
                    arrived(step, 1, par, j)

    def pick(near, n):
        return jnp.where(n == 0, near[0], jnp.where(n == 1, near[3], jnp.where(n == 2, near[1], near[2])))

    def attend(i, carry):
        events_at(i)
        slot, half = i // 2, i % 2
        xa, xb = pick(near_x, 2 * half), pick(near_x, 2 * half + 1)
        ya = yb = pick(near_y, slot)

        @pl.when((slot < 3) & (i > 0) & (i != 4))
        def _():
            for j in both_j:
                arrived_at(xa, ya, opp, j)

        @pl.when(i == 7)
        def _():
            for j in both_j:
                arrived_at(xa, ya, par, j)
                arrived_at(xa, ya, opp, j)

        for j in both_j:
            arrived_at(xb, yb, opp, j)

        @pl.when(slot == 3)
        def _():
            for j in both_j:
                arrived_at(xb, yb, par, j)

        queries = qs[...]
        best = top[...]
        for n, (a, b) in enumerate(((xa, ya), (xb, yb))):
            keys = jnp.concatenate([kv[a, b, 0, 0][:SPLIT], kv[a, b, 1, 0]], axis=0)
            found = lax.dot_general(
                keys, queries, (((1,), (1,)), ((), ())), preferred_element_type=jnp.float32
            )
            scores[n] = found
            best = jnp.maximum(best, jnp.max(found, axis=0, keepdims=True) + bias[pl.ds(a, 1), :])
        scale = jnp.exp(top[...] - best)
        top[...] = best
        row_sum = total[...] * scale
        added = acc[...] * scale
        for n, (a, b) in enumerate(((xa, ya), (xb, yb))):
            weights = jnp.exp(scores[n] + jnp.where(bias[pl.ds(a, 1), :] < 0, MASKED_SCORE, -best))
            row_sum = row_sum + jnp.sum(weights, axis=0, keepdims=True)
            values = jnp.concatenate([kv[a, b, 0, 1][:SPLIT], kv[a, b, 1, 1]], axis=0)
            added = added + lax.dot_general(
                values, weights.astype(jnp.bfloat16), (((0,), (0,)), ((), ())), preferred_element_type=jnp.float32
            )
        total[...] = row_sum
        acc[...] = added
        return carry

    lax.fori_loop(0, 8, attend, 0)

    has_any = jnp.max(bias[0:n_x, :], axis=0, keepdims=True) > 0.5 * MASKED_SCORE
    divided = acc[...] / jnp.where(has_any, total[...], 1.0)
    context = jnp.where(has_any, divided, 0.0)
    for h in range(heads):
        out_ref[:, h * HD : (h + 1) * HD] = context[:, h * HD : (h + 1) * HD].T.astype(jnp.bfloat16)

    for copy in sent:
        copy.wait_send()
    for i, j in enumerate(flying):
        chunk(0, 0, 0, j, kv_send.at[i], z_pair).wait_send()


def solution(mesh):
    n_x = n_y = 4
    n_t = mesh.shape["tensor"]
    names = mesh.axis_names
    strides = tuple((name, math.prod(mesh.shape[m] for m in names[i + 1 :])) for i, name in enumerate(names))

    def on_device(queries, images, kv_weight, q_gain, k_gain, tile_mask):
        tokens, width = queries.shape
        rows, depth = images.shape[1:]
        heads = width // HD
        groups = mesh.shape["dp"]
        any_space = pl.BlockSpec(memory_space=pltpu.HBM)
        vmem = pl.BlockSpec(memory_space=pltpu.VMEM)
        dma = pltpu.SemaphoreType.DMA
        return pl.pallas_call(
            functools.partial(kernel, (n_x, n_y, n_t, heads, strides)),
            out_shape=jax.ShapeDtypeStruct((tokens, width), jnp.bfloat16),
            in_specs=[any_space] * 6,
            out_specs=vmem,
            scratch_shapes=[
                pltpu.VMEM((rows, depth), jnp.bfloat16),
                pltpu.VMEM((groups, *kv_weight.shape), jnp.bfloat16),
                pltpu.VMEM((tokens, width), jnp.bfloat16),
                pltpu.VMEM((1, HD), jnp.float32),
                pltpu.VMEM((1, HD), jnp.float32),
                pltpu.VMEM((n_x, tokens), jnp.int32),
                pltpu.VMEM((width, HD), jnp.bfloat16),
                pltpu.VMEM((8, width), jnp.float32),
                pltpu.VMEM((n_t // 2, 2, rows, HD), jnp.bfloat16),
                pltpu.VMEM((n_t // 2, 2, UNIT, HD), jnp.bfloat16),
                pltpu.VMEM((n_t // 2 - 1, 2, UNIT, HD), jnp.bfloat16),
                pltpu.VMEM((n_x, n_y, 2, 2, UNIT, HD), jnp.bfloat16),
                pltpu.VMEM((2, rows, width), jnp.float32),
                pltpu.VMEM((HD, width), jnp.float32),
                pltpu.VMEM((1, width), jnp.float32),
                pltpu.VMEM((1, width), jnp.float32),
                dma((6,)), dma((3, 2, 2)), dma((3, 2, 2)),
                dma((n_t // 2, 2)), dma((n_t // 2, 2)),
                dma((n_t // 2 - 1, 2)), dma((n_t // 2 - 1, 2)),
                dma((n_x, n_y, 2, 2)), dma((SENDS,)),
            ],
            compiler_params=pltpu.CompilerParams(
                collective_id=0, has_side_effects=True, vmem_limit_bytes=67043328
            ),
        )(images, kv_weight, queries, q_gain.reshape(1, HD), k_gain.reshape(1, HD), tile_mask.T)

    in_specs = (
        P(("section", "dp"), "tensor"),
        P("dp", "section", "tensor"),
        P(None, "tensor", "dp"),
        P(),
        P(),
        P(("section", "dp"), None),
    )
    out_specs = P(("section", "dp"), "tensor")
    return jax.shard_map(on_device, mesh=mesh, in_specs=in_specs, out_specs=out_specs, check_vma=False)
```

```python
import functools
import math

import jax
import jax.numpy as jnp
from jax import lax
from jax.experimental import pallas as pl
from jax.experimental.pallas import tpu as pltpu
from jax.sharding import PartitionSpec as P

EPSILON = 1e-05
MASKED_SCORE = -1e30
LOGICAL = pl.DeviceIdType.LOGICAL
HD = 128
SPLIT = 96
UNIT = 104
SENDS = 72


def kernel(
    dims,
    img_hbm, w_hbm, q_hbm, qg_hbm, kg_hbm, mask_hbm,
    out_ref,
    img, wbuf, qbuf, qg_ref, kg_ref, mask_ref, qs, bias, part, rp, rm, kv, scores, acc, top, total,
    load_sem, w_send, w_recv, p_send, p_recv, m_send, m_recv, kv_recv, kv_send,
):
    n_x, n_y, n_t, heads, strides = dims
    strides = dict(strides)
    half_ring = n_t // 2
    s, d, t = lax.axis_index("section"), lax.axis_index("dp"), lax.axis_index("tensor")
    x, yh = s // n_y, s % n_y
    yl, core = d // 2, d % 2
    par = t % 2

    def wrap(value, size):
        return jnp.where(value >= size, value - size, value)

    near_x = tuple(wrap(x + step, n_x) for step in range(4))
    near_y = tuple(wrap(yh + step, n_y) for step in range(4))

    def device(a=0, b=0, dp=None, tensor=None):
        section = near_x[a % 4] * n_y + near_y[b % 4]
        dp, tensor = d if dp is None else dp, t if tensor is None else tensor
        return section * strides["section"] + dp * strides["dp"] + tensor * strides["tensor"]

    other, far = d + 1 - 2 * core, (1 - yl) * 2 + core
    across = (1 - yl) * 2 + 1 - core
    low_side = device(dp=far)
    partner = device(dp=other)
    y_next = jnp.where(yl == 0, low_side, device(b=1, dp=far))
    y_prev = jnp.where(yl == 1, low_side, device(b=-1, dp=far))
    z_at = {step: device(tensor=wrap(t + step % n_t, n_t)) for step in (-2, -1, 1, 2)}
    z_pair = device(tensor=t + 1 - 2 * par)
    y_group = tuple(device(b=step) for step in (-1, 1, 2))
    x_group = tuple(device(a=step) for step in (-1, 1, 2))

    def remote(src, dst, send, recv, where):
        return pltpu.make_async_remote_copy(
            src_ref=src, dst_ref=dst, send_sem=send, recv_sem=recv, device_id=where, device_id_type=LOGICAL
        )

    loads = [
        pltpu.make_async_copy(src, dst, load_sem.at[i])
        for i, (src, dst) in enumerate(
            (
                (img_hbm.at[0], img),
                (w_hbm, wbuf.at[d]),
                (q_hbm, qbuf),
                (qg_hbm, qg_ref),
                (mask_hbm, mask_ref),
                (kg_hbm, kg_ref),
            )
        )
    ]
    for load in loads:
        load.start()

    barrier = pltpu.get_barrier_semaphore()
    near = (partner, y_next, y_prev, *z_at.values(), *y_group, *x_group)
    for where in near:
        pl.semaphore_signal(barrier, inc=1, device_id=where, device_id_type=LOGICAL)
    pl.semaphore_wait(barrier, len(near))

    depth = img.shape[1] // 2

    def halves(group, j, stage):
        rows = (pl.ds(0, depth), pl.ds(depth, depth))
        return [(wbuf.at[group, j, rows[i], :], w_send.at[stage, j, i], w_recv.at[stage, j, i]) for i in range(2)]

    sent = []

    def launch(copy):
        copy.start()
        sent.append(copy)

    for j in range(2):
        for i, where in enumerate((y_next, y_prev)):
            dst, send, recv = halves(d, j, 0)[i]
            launch(remote(w_hbm.at[j, pl.ds(i * depth, depth), :], dst, send, recv, where))
        launch(remote(w_hbm.at[j], wbuf.at[d, j], w_send.at[2, j, 0], w_recv.at[2, j, 0], partner))

    loads[0].wait()
    loads[1].wait()
    features = img[...]

    def project(group, j):
        both = jnp.dot(features, wbuf[group, j], preferred_element_type=jnp.float32).astype(jnp.bfloat16)
        part[2 * group, j] = both[:, :HD]
        part[2 * group + 1, j] = both[:, HD:]

    project(d, 0)
    project(d, 1)

    for load in loads[2:]:
        load.wait()
    for h in range(heads):
        rows = qbuf[:, h * HD : (h + 1) * HD].astype(jnp.float32)
        mean_sq = jnp.mean(rows * rows, axis=-1, keepdims=True)
        normed = rows * lax.rsqrt(mean_sq + EPSILON) * qg_ref[...] * HD ** (-0.5)
        qs[h * HD : (h + 1) * HD, :] = normed.astype(jnp.bfloat16)
    hidden = jnp.where(mask_ref[...] > 0, 0.0, MASKED_SCORE)
    for h in range(heads):
        bias[0:n_x, h * HD : (h + 1) * HD] = hidden
    top[...] = jnp.full_like(top, MASKED_SCORE)
    total[...] = jnp.zeros_like(total)
    acc[...] = jnp.zeros_like(acc)

    for j in range(2):
        remote(w_hbm.at[j], wbuf.at[other, j], w_send.at[2, j, 0], w_recv.at[2, j, 0], partner).wait_recv()
        project(other, j)

    def far_weights(j):
        for (dst, send, recv), (_, send_on, recv_on) in zip(halves(far, j, 0), halves(far, j, 1)):
            remote(dst, dst, send, recv, partner).wait_recv()
            launch(remote(dst, dst, send_on, recv_on, partner))
        project(far, j)
        for dst, send, recv in halves(across, j, 1):
            remote(dst, dst, send, recv, partner).wait_recv()
        project(across, j)

    pair, heads_kv = t // 2, n_t // 2

    def own_part(offset, j):
        offset %= n_t
        odd = offset % 2
        start = (1 - par if odd else par) * SPLIT
        head = wrap(pair + offset // 2 + (par if odd else 0), heads_kv)
        return part.at[head, j, pl.ds(pl.multiple_of(start, 16), UNIT), :]

    rings = ((1, half_ring, rp, p_send, p_recv), (-1, half_ring - 1, rm, m_send, m_recv))

    def hop(ring, offset, j, src):
        sign, _, buf, send, recv = rings[ring]
        jump = 2 - offset % 2
        return remote(src, buf.at[offset - 1, j], send.at[offset - 1, j], recv.at[offset - 1, j], z_at[sign * jump])

    def send_sum(ring, offset, j):
        sign, longest, buf, send, recv = rings[ring]
        own = own_part(sign * offset, j)
        src = own
        if offset % 2 == 0 and offset < longest:
            rows = own[...].astype(jnp.float32)
            for before in (offset + 1, offset + 2):
                if before <= longest:
                    got = buf.at[before - 1, j]
                    hop(ring, before, j, got).wait_recv()
                    rows = rows + got[...].astype(jnp.float32)
            src = buf.at[offset + 1 if offset + 2 <= longest else offset, j]
            src[...] = rows.astype(jnp.bfloat16)
        launch(hop(ring, offset, j, src))

    for offset in range(half_ring, 0, -2):
        for j in range(2):
            if offset == half_ring:
                far_weights(j)
            for ring in range(2):
                for now in (offset, offset - 1):
                    if now <= rings[ring][1]:
                        send_sum(ring, now, j)

    def finish(j):
        rows = own_part(0, j)[...].astype(jnp.float32)
        for ring in range(2):
            for offset in (1, 2):
                got = rings[ring][2].at[offset - 1, j]
                hop(ring, offset, j, got).wait_recv()
                rows = rows + got[...].astype(jnp.float32)
        if j == 0:
            mean_sq = jnp.mean(rows * rows, axis=-1, keepdims=True)
            rows = rows * lax.rsqrt(mean_sq + EPSILON) * kg_ref[...]
        kv[x, yh, par, j] = rows.astype(jnp.bfloat16)

    flying = []

    def chunk_at(a, b, q, j, send, where):
        return remote(kv.at[a, b, q, j], kv.at[a, b, q, j], send, kv_recv.at[a, b, q, j], where)

    def chunk(a, b, q, j, send, where):
        return chunk_at(near_x[a % 4], near_y[b % 4], q, j, send, where)

    def arrived(a, b, q, j):
        chunk(a, b, q, j, kv_send.at[0], z_pair).wait_recv()

    def arrived_at(a, b, q, j):
        chunk_at(a, b, q, j, kv_send.at[0], z_pair).wait_recv()

    def forward(a, b, q, j, *where):
        for device in where:
            chunk(a, b, q, j, kv_send.at[len(flying)], device).start()
            flying.append(j)

    both_j = (0, 1)
    opp = 1 - par
    for j in both_j:
        finish(j)
        forward(0, 0, par, j, z_pair, *y_group, *x_group)
    for j in both_j:
        arrived(0, 0, opp, j)
        forward(0, 0, opp, j, *y_group[:2], *x_group)
    for j in both_j:
        for step in (-1, 1, 2):
            arrived(step, 0, par, j)
    for slot in (-1, 1, 2):
        for j in both_j:
            arrived(0, slot, par, j)
            forward(0, slot, par, j, *((z_pair, *x_group) if slot == 2 else x_group))

    def events_at(i):
        @pl.when(i == 2)
        def _():
            for j in both_j:
                for step in (-1, 1, 2):
                    arrived(step, -1, par, j)
                    forward(step, -1, par, j, z_pair)
            for slot in (1, 2):
                for j in both_j:
                    arrived(0, slot, opp, j)
                    if slot == 2:
                        forward(0, slot, opp, j, *x_group)
            for j in both_j:
                for step in (-1, 1, 2):
                    arrived(step, 1, par, j)
                    forward(step, 1, par, j, z_pair)

    def pick(near, n):
        return jnp.where(n == 0, near[0], jnp.where(n == 1, near[3], jnp.where(n == 2, near[1], near[2])))

    def attend(i, carry):
        events_at(i)
        slot, half = i // 2, i % 2
        xa, xb = pick(near_x, 2 * half), pick(near_x, 2 * half + 1)
        ya = yb = pick(near_y, slot)

        @pl.when((slot < 3) & (i > 0) & (i != 4))
        def _():
            for j in both_j:
                arrived_at(xa, ya, opp, j)

        @pl.when(i == 7)
        def _():
            for j in both_j:
                arrived_at(xa, ya, par, j)
                arrived_at(xa, ya, opp, j)

        for j in both_j:
            arrived_at(xb, yb, opp, j)

        @pl.when(slot == 3)
        def _():
            for j in both_j:
                arrived_at(xb, yb, par, j)

        queries = qs[...]
        best = top[...]
        for n, (a, b) in enumerate(((xa, ya), (xb, yb))):
            keys = jnp.concatenate([kv[a, b, 0, 0][:SPLIT], kv[a, b, 1, 0]], axis=0)
            found = lax.dot_general(
                keys, queries, (((1,), (1,)), ((), ())), preferred_element_type=jnp.float32
            )
            scores[n] = found
            best = jnp.maximum(best, jnp.max(found, axis=0, keepdims=True) + bias[pl.ds(a, 1), :])
        scale = jnp.exp(top[...] - best)
        top[...] = best
        row_sum = total[...] * scale
        added = acc[...] * scale
        for n, (a, b) in enumerate(((xa, ya), (xb, yb))):
            weights = jnp.exp(scores[n] + jnp.where(bias[pl.ds(a, 1), :] < 0, MASKED_SCORE, -best))
            row_sum = row_sum + jnp.sum(weights, axis=0, keepdims=True)
            values = jnp.concatenate([kv[a, b, 0, 1][:SPLIT], kv[a, b, 1, 1]], axis=0)
            added = added + lax.dot_general(
                values, weights.astype(jnp.bfloat16), (((0,), (0,)), ((), ())), preferred_element_type=jnp.float32
            )
        total[...] = row_sum
        acc[...] = added
        return carry

    lax.fori_loop(0, 8, attend, 0)

    has_any = jnp.max(bias[0:n_x, :], axis=0, keepdims=True) > 0.5 * MASKED_SCORE
    divided = acc[...] / jnp.where(has_any, total[...], 1.0)
    context = jnp.where(has_any, divided, 0.0)
    for h in range(heads):
        out_ref[:, h * HD : (h + 1) * HD] = context[:, h * HD : (h + 1) * HD].T.astype(jnp.bfloat16)

    for copy in sent:
        copy.wait_send()
    for i, j in enumerate(flying):
        chunk(0, 0, 0, j, kv_send.at[i], z_pair).wait_send()


def solution(mesh):
    n_x = n_y = 4
    n_t = mesh.shape["tensor"]
    names = mesh.axis_names
    strides = tuple((name, math.prod(mesh.shape[m] for m in names[i + 1 :])) for i, name in enumerate(names))

    def on_device(queries, images, kv_weight, q_gain, k_gain, tile_mask):
        tokens, width = queries.shape
        rows, depth = images.shape[1:]
        heads = width // HD
        groups = mesh.shape["dp"]
        any_space = pl.BlockSpec(memory_space=pltpu.HBM)
        vmem = pl.BlockSpec(memory_space=pltpu.VMEM)
        dma = pltpu.SemaphoreType.DMA
        return pl.pallas_call(
            functools.partial(kernel, (n_x, n_y, n_t, heads, strides)),
            out_shape=jax.ShapeDtypeStruct((tokens, width), jnp.bfloat16),
            in_specs=[any_space] * 6,
            out_specs=vmem,
            scratch_shapes=[
                pltpu.VMEM((rows, depth), jnp.bfloat16),
                pltpu.VMEM((groups, *kv_weight.shape), jnp.bfloat16),
                pltpu.VMEM((tokens, width), jnp.bfloat16),
                pltpu.VMEM((1, HD), jnp.float32),
                pltpu.VMEM((1, HD), jnp.float32),
                pltpu.VMEM((n_x, tokens), jnp.int32),
                pltpu.VMEM((width, HD), jnp.bfloat16),
                pltpu.VMEM((8, width), jnp.float32),
                pltpu.VMEM((n_t // 2, 2, rows, HD), jnp.bfloat16),
                pltpu.VMEM((n_t // 2, 2, UNIT, HD), jnp.bfloat16),
                pltpu.VMEM((n_t // 2 - 1, 2, UNIT, HD), jnp.bfloat16),
                pltpu.VMEM((n_x, n_y, 2, 2, UNIT, HD), jnp.bfloat16),
                pltpu.VMEM((2, rows, width), jnp.float32),
                pltpu.VMEM((HD, width), jnp.float32),
                pltpu.VMEM((1, width), jnp.float32),
                pltpu.VMEM((1, width), jnp.float32),
                dma((6,)), dma((3, 2, 2)), dma((3, 2, 2)),
                dma((n_t // 2, 2)), dma((n_t // 2, 2)),
                dma((n_t // 2 - 1, 2)), dma((n_t // 2 - 1, 2)),
                dma((n_x, n_y, 2, 2)), dma((SENDS,)),
            ],
            compiler_params=pltpu.CompilerParams(
                collective_id=0, has_side_effects=True, vmem_limit_bytes=67043328
            ),
        )(images, kv_weight, queries, q_gain.reshape(1, HD), k_gain.reshape(1, HD), tile_mask.T)

    in_specs = (
        P(("section", "dp"), "tensor"),
        P("dp", "section", "tensor"),
        P(None, "tensor", "dp"),
        P(),
        P(),
        P(("section", "dp"), None),
    )
    out_specs = P(("section", "dp"), "tensor")
    return jax.shard_map(on_device, mesh=mesh, in_specs=in_specs, out_specs=out_specs, check_vma=False)
```

```python
import functools
import math

import jax
import jax.numpy as jnp
from jax import lax
from jax.experimental import pallas as pl
from jax.experimental.pallas import tpu as pltpu
from jax.sharding import PartitionSpec as P

EPSILON = 1e-05
MASKED_SCORE = -1e30
LOGICAL = pl.DeviceIdType.LOGICAL
HD = 128
SPLIT = 96
UNIT = 104
SENDS = 72


def kernel(
    dims,
    img_hbm, w_hbm, q_hbm, qg_hbm, kg_hbm, mask_hbm,
    out_ref,
    img, wbuf, qbuf, qg_ref, kg_ref, mask_ref, qs, bias, part, rp, rm, kv, scores, acc, top, total,
    load_sem, w_send, w_recv, p_send, p_recv, m_send, m_recv, kv_recv, kv_send,
):
    n_x, n_y, n_t, heads, strides = dims
    strides = dict(strides)
    half_ring = n_t // 2
    s, d, t = lax.axis_index("section"), lax.axis_index("dp"), lax.axis_index("tensor")
    x, yh = s // n_y, s % n_y
    yl, core = d // 2, d % 2
    par = t % 2

    def wrap(value, size):
        return jnp.where(value >= size, value - size, value)

    near_x = tuple(wrap(x + step, n_x) for step in range(4))
    near_y = tuple(wrap(yh + step, n_y) for step in range(4))

    def device(a=0, b=0, dp=None, tensor=None):
        section = near_x[a % 4] * n_y + near_y[b % 4]
        dp, tensor = d if dp is None else dp, t if tensor is None else tensor
        return section * strides["section"] + dp * strides["dp"] + tensor * strides["tensor"]

    other, far = d + 1 - 2 * core, (1 - yl) * 2 + core
    across = (1 - yl) * 2 + 1 - core
    low_side = device(dp=far)
    partner = device(dp=other)
    y_next = jnp.where(yl == 0, low_side, device(b=1, dp=far))
    y_prev = jnp.where(yl == 1, low_side, device(b=-1, dp=far))
    z_at = {step: device(tensor=wrap(t + step % n_t, n_t)) for step in (-2, -1, 1, 2)}
    z_pair = device(tensor=t + 1 - 2 * par)
    y_group = tuple(device(b=step) for step in (-1, 1, 2))
    x_group = tuple(device(a=step) for step in (-1, 1, 2))

    def remote(src, dst, send, recv, where):
        return pltpu.make_async_remote_copy(
            src_ref=src, dst_ref=dst, send_sem=send, recv_sem=recv, device_id=where, device_id_type=LOGICAL
        )

    loads = [
        pltpu.make_async_copy(src, dst, load_sem.at[i])
        for i, (src, dst) in enumerate(
            (
                (img_hbm.at[0], img),
                (w_hbm, wbuf.at[d]),
                (q_hbm, qbuf),
                (qg_hbm, qg_ref),
                (mask_hbm, mask_ref),
                (kg_hbm, kg_ref),
            )
        )
    ]
    for load in loads:
        load.start()

    barrier = pltpu.get_barrier_semaphore()
    near = (partner, y_next, y_prev, *z_at.values(), *y_group, *x_group)
    for where in near:
        pl.semaphore_signal(barrier, inc=1, device_id=where, device_id_type=LOGICAL)
    pl.semaphore_wait(barrier, len(near))

    depth = img.shape[1] // 2

    def halves(group, j, stage):
        rows = (pl.ds(0, depth), pl.ds(depth, depth))
        return [(wbuf.at[group, j, rows[i], :], w_send.at[stage, j, i], w_recv.at[stage, j, i]) for i in range(2)]

    sent = []

    def launch(copy):
        copy.start()
        sent.append(copy)

    for j in range(2):
        for i, where in enumerate((y_next, y_prev)):
            dst, send, recv = halves(d, j, 0)[i]
            launch(remote(w_hbm.at[j, pl.ds(i * depth, depth), :], dst, send, recv, where))
        launch(remote(w_hbm.at[j], wbuf.at[d, j], w_send.at[2, j, 0], w_recv.at[2, j, 0], partner))

    loads[0].wait()
    loads[1].wait()
    features = img[...]

    def project(group, j):
        both = jnp.dot(features, wbuf[group, j], preferred_element_type=jnp.float32).astype(jnp.bfloat16)
        part[2 * group, j] = both[:, :HD]
        part[2 * group + 1, j] = both[:, HD:]

    project(d, 0)
    project(d, 1)

    for load in loads[2:]:
        load.wait()
    for h in range(heads):
        rows = qbuf[:, h * HD : (h + 1) * HD].astype(jnp.float32)
        mean_sq = jnp.mean(rows * rows, axis=-1, keepdims=True)
        normed = rows * lax.rsqrt(mean_sq + EPSILON) * qg_ref[...] * HD ** (-0.5)
        qs[h * HD : (h + 1) * HD, :] = normed.astype(jnp.bfloat16)
    hidden = jnp.where(mask_ref[...] > 0, 0.0, MASKED_SCORE)
    for h in range(heads):
        bias[0:n_x, h * HD : (h + 1) * HD] = hidden
    top[...] = jnp.full_like(top, MASKED_SCORE)
    total[...] = jnp.zeros_like(total)
    acc[...] = jnp.zeros_like(acc)

    for j in range(2):
        remote(w_hbm.at[j], wbuf.at[other, j], w_send.at[2, j, 0], w_recv.at[2, j, 0], partner).wait_recv()
        project(other, j)

    def far_weights(j):
        for (dst, send, recv), (_, send_on, recv_on) in zip(halves(far, j, 0), halves(far, j, 1)):
            remote(dst, dst, send, recv, partner).wait_recv()
            launch(remote(dst, dst, send_on, recv_on, partner))
        project(far, j)
        for dst, send, recv in halves(across, j, 1):
            remote(dst, dst, send, recv, partner).wait_recv()
        project(across, j)

    pair, heads_kv = t // 2, n_t // 2

    def own_part(offset, j):
        offset %= n_t
        odd = offset % 2
        start = (1 - par if odd else par) * SPLIT
        head = wrap(pair + offset // 2 + (par if odd else 0), heads_kv)
        return part.at[head, j, pl.ds(pl.multiple_of(start, 16), UNIT), :]

    rings = ((1, half_ring, rp, p_send, p_recv), (-1, half_ring - 1, rm, m_send, m_recv))

    def hop(ring, offset, j, src):
        sign, _, buf, send, recv = rings[ring]
        jump = 2 - offset % 2
        return remote(src, buf.at[offset - 1, j], send.at[offset - 1, j], recv.at[offset - 1, j], z_at[sign * jump])

    def send_sum(ring, offset, j):
        sign, longest, buf, send, recv = rings[ring]
        own = own_part(sign * offset, j)
        src = own
        if offset % 2 == 0 and offset < longest:
            rows = own[...].astype(jnp.float32)
            for before in (offset + 1, offset + 2):
                if before <= longest:
                    got = buf.at[before - 1, j]
                    hop(ring, before, j, got).wait_recv()
                    rows = rows + got[...].astype(jnp.float32)
            src = buf.at[offset + 1 if offset + 2 <= longest else offset, j]
            src[...] = rows.astype(jnp.bfloat16)
        launch(hop(ring, offset, j, src))

    for offset in range(half_ring, 0, -2):
        for j in range(2):
            if offset == half_ring:
                far_weights(j)
            for ring in range(2):
                for now in (offset, offset - 1):
                    if now <= rings[ring][1]:
                        send_sum(ring, now, j)

    def finish(j):
        rows = own_part(0, j)[...].astype(jnp.float32)
        for ring in range(2):
            for offset in (1, 2):
                got = rings[ring][2].at[offset - 1, j]
                hop(ring, offset, j, got).wait_recv()
                rows = rows + got[...].astype(jnp.float32)
        if j == 0:
            mean_sq = jnp.mean(rows * rows, axis=-1, keepdims=True)
            rows = rows * lax.rsqrt(mean_sq + EPSILON) * kg_ref[...]
        kv[x, yh, par, j] = rows.astype(jnp.bfloat16)

    flying = []

    def chunk_at(a, b, q, j, send, where):
        return remote(kv.at[a, b, q, j], kv.at[a, b, q, j], send, kv_recv.at[a, b, q, j], where)

    def chunk(a, b, q, j, send, where):
        return chunk_at(near_x[a % 4], near_y[b % 4], q, j, send, where)

    def arrived(a, b, q, j):
        chunk(a, b, q, j, kv_send.at[0], z_pair).wait_recv()

    def arrived_at(a, b, q, j):
        chunk_at(a, b, q, j, kv_send.at[0], z_pair).wait_recv()

    def forward(a, b, q, j, *where):
        for device in where:
            chunk(a, b, q, j, kv_send.at[len(flying)], device).start()
            flying.append(j)

    both_j = (0, 1)
    opp = 1 - par
    for j in both_j:
        finish(j)
        forward(0, 0, par, j, z_pair, *y_group, *x_group)
    for j in both_j:
        arrived(0, 0, opp, j)
        forward(0, 0, opp, j, *y_group[:2], *x_group)
    for j in both_j:
        for step in (-1, 1, 2):
            arrived(step, 0, par, j)
    for slot in (-1, 1, 2):
        for j in both_j:
            arrived(0, slot, par, j)
            forward(0, slot, par, j, *((z_pair, *x_group) if slot == 2 else x_group))

    def events_at(i):
        @pl.when(i == 1)
        def _():
            for slot in (-1, 1):
                for j in both_j:
                    for step in (-1, 1, 2):
                        arrived(step, slot, par, j)
                        forward(step, slot, par, j, z_pair)

        @pl.when(i == 2)
        def _():
            for slot in (1, 2):
                for j in both_j:
                    arrived(0, slot, opp, j)
                    if slot == 2:
                        forward(0, slot, opp, j, *x_group)

    def pick(near, n):
        return jnp.where(n == 0, near[0], jnp.where(n == 1, near[3], jnp.where(n == 2, near[1], near[2])))

    def attend(i, carry):
        events_at(i)
        slot, half = i // 2, i % 2
        xa, xb = pick(near_x, 2 * half), pick(near_x, 2 * half + 1)
        ya = yb = pick(near_y, slot)

        @pl.when((slot < 3) & (i > 0) & (i != 4))
        def _():
            for j in both_j:
                arrived_at(xa, ya, opp, j)

        @pl.when(i == 7)
        def _():
            for j in both_j:
                arrived_at(xa, ya, par, j)
                arrived_at(xa, ya, opp, j)

        for j in both_j:
            arrived_at(xb, yb, opp, j)

        @pl.when(slot == 3)
        def _():
            for j in both_j:
                arrived_at(xb, yb, par, j)

        queries = qs[...]
        best = top[...]
        for n, (a, b) in enumerate(((xa, ya), (xb, yb))):
            keys = jnp.concatenate([kv[a, b, 0, 0][:SPLIT], kv[a, b, 1, 0]], axis=0)
            found = lax.dot_general(
                keys, queries, (((1,), (1,)), ((), ())), preferred_element_type=jnp.float32
            )
            scores[n] = found
            best = jnp.maximum(best, jnp.max(found, axis=0, keepdims=True) + bias[pl.ds(a, 1), :])
        scale = jnp.exp(top[...] - best)
        top[...] = best
        row_sum = total[...] * scale
        added = acc[...] * scale
        for n, (a, b) in enumerate(((xa, ya), (xb, yb))):
            weights = jnp.exp(scores[n] + jnp.where(bias[pl.ds(a, 1), :] < 0, MASKED_SCORE, -best))
            row_sum = row_sum + jnp.sum(weights, axis=0, keepdims=True)
            values = jnp.concatenate([kv[a, b, 0, 1][:SPLIT], kv[a, b, 1, 1]], axis=0)
            added = added + lax.dot_general(
                values, weights.astype(jnp.bfloat16), (((0,), (0,)), ((), ())), preferred_element_type=jnp.float32
            )
        total[...] = row_sum
        acc[...] = added
        return carry

    lax.fori_loop(0, 8, attend, 0)

    has_any = jnp.max(bias[0:n_x, :], axis=0, keepdims=True) > 0.5 * MASKED_SCORE
    divided = acc[...] / jnp.where(has_any, total[...], 1.0)
    context = jnp.where(has_any, divided, 0.0)
    for h in range(heads):
        out_ref[:, h * HD : (h + 1) * HD] = context[:, h * HD : (h + 1) * HD].T.astype(jnp.bfloat16)

    for copy in sent:
        copy.wait_send()
    for i, j in enumerate(flying):
        chunk(0, 0, 0, j, kv_send.at[i], z_pair).wait_send()


def solution(mesh):
    n_x = n_y = 4
    n_t = mesh.shape["tensor"]
    names = mesh.axis_names
    strides = tuple((name, math.prod(mesh.shape[m] for m in names[i + 1 :])) for i, name in enumerate(names))

    def on_device(queries, images, kv_weight, q_gain, k_gain, tile_mask):
        tokens, width = queries.shape
        rows, depth = images.shape[1:]
        heads = width // HD
        groups = mesh.shape["dp"]
        any_space = pl.BlockSpec(memory_space=pltpu.HBM)
        vmem = pl.BlockSpec(memory_space=pltpu.VMEM)
        dma = pltpu.SemaphoreType.DMA
        return pl.pallas_call(
            functools.partial(kernel, (n_x, n_y, n_t, heads, strides)),
            out_shape=jax.ShapeDtypeStruct((tokens, width), jnp.bfloat16),
            in_specs=[any_space] * 6,
            out_specs=vmem,
            scratch_shapes=[
                pltpu.VMEM((rows, depth), jnp.bfloat16),
                pltpu.VMEM((groups, *kv_weight.shape), jnp.bfloat16),
                pltpu.VMEM((tokens, width), jnp.bfloat16),
                pltpu.VMEM((1, HD), jnp.float32),
                pltpu.VMEM((1, HD), jnp.float32),
                pltpu.VMEM((n_x, tokens), jnp.int32),
                pltpu.VMEM((width, HD), jnp.bfloat16),
                pltpu.VMEM((8, width), jnp.float32),
                pltpu.VMEM((n_t // 2, 2, rows, HD), jnp.bfloat16),
                pltpu.VMEM((n_t // 2, 2, UNIT, HD), jnp.bfloat16),
                pltpu.VMEM((n_t // 2 - 1, 2, UNIT, HD), jnp.bfloat16),
                pltpu.VMEM((n_x, n_y, 2, 2, UNIT, HD), jnp.bfloat16),
                pltpu.VMEM((2, rows, width), jnp.float32),
                pltpu.VMEM((HD, width), jnp.float32),
                pltpu.VMEM((1, width), jnp.float32),
                pltpu.VMEM((1, width), jnp.float32),
                dma((6,)), dma((3, 2, 2)), dma((3, 2, 2)),
                dma((n_t // 2, 2)), dma((n_t // 2, 2)),
                dma((n_t // 2 - 1, 2)), dma((n_t // 2 - 1, 2)),
                dma((n_x, n_y, 2, 2)), dma((SENDS,)),
            ],
            compiler_params=pltpu.CompilerParams(
                collective_id=0, has_side_effects=True, vmem_limit_bytes=67043328
            ),
        )(images, kv_weight, queries, q_gain.reshape(1, HD), k_gain.reshape(1, HD), tile_mask.T)

    in_specs = (
        P(("section", "dp"), "tensor"),
        P("dp", "section", "tensor"),
        P(None, "tensor", "dp"),
        P(),
        P(),
        P(("section", "dp"), None),
    )
    out_specs = P(("section", "dp"), "tensor")
    return jax.shard_map(on_device, mesh=mesh, in_specs=in_specs, out_specs=out_specs, check_vma=False)
```
